256 devices in a mesh: row: 16 (over x_hi, y, core), col: 16 (over z, x_lo).
Axes of the slice: x: 4 (x_hi: 2, x_lo: 2; x = x_hi * 2 + x_lo), y: 4, z: 8, core: 2. Of those that a mesh axis runs over, the one named last changes fastest.
Arguments:
- vectors: float32 [16, 32768], P(None, ('col', 'row')), may hold values from -6 to 6
- tile_blocks: float32 [16, 16, 128, 128, 128], P('row', 'col'), may hold values from -0.046875 to 0.046875
- coords: int32 [16, 16, 128], P('row', 'col'), may hold values from 0 to 255, as said below
- counts: int32 [16, 16], P('row', 'col'), may hold values from 1 to 128, as said below
Outputs:
- product: float32 [16, 32768], P(None, ('col', 'row'))
The draws below stay inside these ranges and needn't reach their ends.
Inputs may be any that keep to these rules, and one draw needn't show every extreme that they name: `counts`: every cell has at least one live slot and some cell has exactly 128. `coords`: within one cell all 128 entries are distinct; slots at or past counts hold no tile of S.
All inputs are finite; a program needn't handle non-finite values.
Results may differ from the reference program's by a relative error of at most 0.0003.
Values sent between devices are 32-bit elements; how exact they have to be, the bound alone decides.
No kernel may reach another device: no remote copies, remote signals or barrier semaphores. Data moves between devices by JAX's collectives and lax.ppermute only.
A program may use at most 64 MiB of HBM per device.

```python
import jax
import jax.numpy as jnp
from jax import lax

NV = 16
TILE = 128
TSEG = 16
TCOL = 16
MAXT = 128
NROWS = 32768
N_ROW = 16
N_COL = 16


def draw_counts(key, part):
    first_key, second_key = jax.random.split(jax.random.fold_in(key, 11))
    drawn_counts = jax.random.randint(first_key, (N_ROW, N_COL), max(1, MAXT // 8), MAXT + 1)
    fullest = jax.random.randint(second_key, (), 0, N_ROW * N_COL)
    device_order = jnp.arange(N_ROW * N_COL, dtype=jnp.int32).reshape(N_ROW, N_COL)
    return jnp.where(device_order == fullest, MAXT, drawn_counts).astype(jnp.int32)


def draw_coords(key, part):
    key_list = jax.random.split(jax.random.fold_in(key, 23), N_ROW * N_COL)
    picked = jax.vmap(lambda one_key: jax.random.permutation(one_key, TSEG * TCOL)[:MAXT])(key_list)
    return picked.reshape(N_ROW, N_COL, MAXT).astype(jnp.int32)


def levels(own_key, shape, pieces, least, largest):
    level = 1.0
    for position, shards_of in pieces:
        draws = jax.random.uniform(jax.random.fold_in(jax.random.fold_in(own_key, 6), position), (shards_of,), jnp.float32, least / len(pieces), largest / len(pieces))
        level = level * jnp.repeat(jnp.exp(draws), shape[position] // shards_of).reshape((-1,) + (1,) * (len(shape) - 1 - position))
    return level


def scatter_about(rng, shape, deviation, bound, pieces=(), kind=jnp.bfloat16):
    drawn = deviation * jax.random.normal(rng, shape, jnp.float32)
    if pieces:
        drawn = drawn * levels(rng, shape, pieces, -0.22, 0.18)
    return jnp.clip(drawn, -bound, bound).astype(kind)


def setup_inputs(seed: int = 0) -> dict:
    seeds = jax.random.split(jax.random.key(seed), 5)
    vectors = scatter_about(seeds[0], (NV, NROWS), 1.0, 6.0, ((1, 256),), jnp.float32)
    tile_blocks = scatter_about(seeds[1], (N_ROW, N_COL, MAXT, TILE, TILE), (TILE * MAXT * N_COL // TSEG) ** -0.5, 0.046875, ((0, 16), (1, 16)), jnp.float32)
    coords = draw_coords(jax.random.fold_in(seeds[4], 71), 0)
    counts = draw_counts(jax.random.fold_in(seeds[4], 71), 0)
    return {"vectors": vectors, "tile_blocks": tile_blocks, "coords": coords, "counts": counts}


HIGH = lax.Precision.HIGHEST


def slot_terms(blocks, slot_coords, live_mask, x_col, x_row):
    vec_count = x_col.shape[0]
    tile_size = blocks.shape[-1]
    seg_tiles = x_row.shape[1] // tile_size
    col_tiles = x_col.shape[1] // tile_size
    row_pos = slot_coords // col_tiles
    col_pos = slot_coords % col_tiles
    picked_col = jnp.take(x_col.reshape(vec_count, col_tiles, tile_size), col_pos, axis=1)
    picked_row = jnp.take(x_row.reshape(vec_count, seg_tiles, tile_size), row_pos, axis=1)
    normal = jnp.einsum("vsk,smk->vsm", picked_col, blocks, precision=HIGH)
    transposed = jnp.einsum("vsm,smk->vsk", picked_row, blocks, precision=HIGH)
    onehot_rows = (row_pos[:, None] == jnp.arange(seg_tiles, dtype=jnp.int32)[None, :]).astype(jnp.float32) * live_mask[:, None]
    onehot_cols = (col_pos[:, None] == jnp.arange(col_tiles, dtype=jnp.int32)[None, :]).astype(jnp.float32) * live_mask[:, None]
    row_terms = jnp.einsum("st,vsm->vtm", onehot_rows, normal, precision=HIGH).reshape(vec_count, seg_tiles * tile_size)
    col_terms = jnp.einsum("st,vsk->vtk", onehot_cols, transposed, precision=HIGH).reshape(vec_count, col_tiles * tile_size)
    return row_terms, col_terms


def reference(vectors, tile_blocks, coords, counts):
    row_len = TSEG * TILE
    col_len = TCOL * TILE
    cells = N_ROW * N_COL
    flat_blocks = tile_blocks.reshape(cells, MAXT, TILE, TILE)
    flat_coords = coords.reshape(cells, MAXT)
    flat_counts = counts.reshape(cells)
    cell_ids = jnp.arange(cells, dtype=jnp.int32)
    slot_ids = jnp.arange(MAXT, dtype=jnp.int32)

    def scan_step(running, scan_items):
        blocks, slot_coords, slot_count, cell_id = scan_items
        row_idx = (cell_id // N_COL).astype(jnp.int32)
        col_idx = (cell_id % N_COL).astype(jnp.int32)
        row_start = (row_idx * row_len).astype(jnp.int32)
        col_start = (col_idx * col_len).astype(jnp.int32)
        x_col = lax.dynamic_slice_in_dim(vectors, col_start, col_len, 1)
        x_row = lax.dynamic_slice_in_dim(vectors, row_start, row_len, 1)
        live_mask = (slot_ids < slot_count).astype(jnp.float32)
        row_terms, col_terms = slot_terms(blocks, slot_coords, live_mask, x_col, x_row)
        current = lax.dynamic_slice_in_dim(running, row_start, row_len, 1)
        running = lax.dynamic_update_slice_in_dim(running, current + row_terms, row_start, 1)
        current = lax.dynamic_slice_in_dim(running, col_start, col_len, 1)
        running = lax.dynamic_update_slice_in_dim(running, current + col_terms, col_start, 1)
        return running, None

    start_value = jnp.zeros((NV, NROWS), jnp.float32)
    product, unused = lax.scan(scan_step, start_value, (flat_blocks, flat_coords, flat_counts, cell_ids))
    return product
```

```python
import jax
import jax.numpy as jnp
from jax import lax
from jax.sharding import PartitionSpec as P

HIGH = lax.Precision.HIGHEST


def local(vectors, tile_blocks, coords, counts):
    n_row = lax.axis_size("row")
    n_col = lax.axis_size("col")
    max_slots = tile_blocks.shape[2]
    tile = tile_blocks.shape[-1]
    vecs = vectors.shape[0]
    flip = [(r * n_col + c, c * n_col + r) for r in range(n_row) for c in range(n_col)]
    blocks = tile_blocks.reshape(max_slots, tile, tile)
    pos = coords.reshape(max_slots)
    live = (jnp.arange(max_slots, dtype=jnp.int32) < counts.reshape(())).astype(jnp.float32)
    row_pos = pos // n_row
    col_pos = pos % n_row
    tiles = jnp.arange(n_row, dtype=jnp.int32)
    pick_row = (row_pos[:, None] == tiles[None, :]).astype(jnp.float32) * live[:, None]
    pick_col = (col_pos[:, None] == tiles[None, :]).astype(jnp.float32) * live[:, None]

    spread = jnp.broadcast_to(vectors[None], (n_row, vecs, tile))
    x_col = lax.all_to_all(spread, "row", 0, 0, tiled=True)
    x_row = lax.ppermute(x_col, ("row", "col"), flip)
    normal = jnp.einsum("svk,smk->svm", jnp.take(x_col, col_pos, axis=0), blocks, precision=HIGH)
    row_terms = jnp.einsum("st,svm->tvm", pick_row, normal, precision=HIGH)
    flipped = lax.ppermute(row_terms, ("row", "col"), flip)
    turned = jnp.einsum("svm,smk->svk", jnp.take(x_row, row_pos, axis=0), blocks, precision=HIGH)
    col_terms = jnp.einsum("st,svk->tvk", pick_col, turned, precision=HIGH)
    parts = lax.all_to_all(col_terms + flipped, "row", 0, 0, tiled=True)
    return jnp.sum(parts, axis=0)


def solution(mesh):
    return jax.shard_map(
        local,
        mesh=mesh,
        in_specs=(
            P(None, ("col", "row")),
            P("row", "col", None, None, None),
            P("row", "col", None),
            P("row", "col"),
        ),
        out_specs=P(None, ("col", "row")),
        check_vma=False,
    )
```

```python
import functools

import jax
import jax.numpy as jnp
from jax import lax
from jax.experimental import pallas as pl
from jax.experimental.pallas import tpu as pltpu
from jax.sharding import PartitionSpec as P

UNROLL = 16
BY_ROWS = (((1,), (0,)), ((), ()))
BY_COLS = (((1,), (1,)), ((), ()))

OUT_TURN = (4, 2, 0, 10, 13, 7, 9, 6, 12, 3, 1, 14, 8, 15, 5, 11)
IN_TURN = (4, 6, 12, 2, 0, 11, 8, 14, 5, 3, 1, 15, 13, 10, 9, 7)


def partner(turn, r, c):
    step = turn[2 * (((c >> 1) - (r >> 1)) % 8) + ((c ^ r) & 1)]
    half = (r >> 3) ^ ((step >> 1) & 1)
    return (half << 3) | ((((r >> 1) + (step >> 2)) & 3) << 1) | (step & 1)


def pairs(turn, n_row, n_col):
    return [
        (r * n_col + c, partner(turn, r, c) * n_col + r) for r in range(n_row) for c in range(n_col)
    ]


def split(value):
    high = value.astype(jnp.bfloat16)
    low = (value - high.astype(jnp.float32)).astype(jnp.bfloat16)
    return high, low


def product_body(rows_out, pos_ref, count_ref, x_ref, tile_ref, out_ref, lhs_ref):
    n_tiles, vecs, _ = x_ref.shape
    for t in range(n_tiles):
        high, low = split(x_ref[t])
        upper = jnp.concatenate([high, high], axis=1)
        lower = jnp.concatenate([low, jnp.zeros_like(low)], axis=1)
        lhs_ref[t] = jnp.concatenate([upper, lower], axis=0)
    lhs_ref[n_tiles] = jnp.zeros(lhs_ref.shape[1:], jnp.bfloat16)
    out_ref[...] = jnp.zeros_like(out_ref)
    count = count_ref[0]

    def group(g, carry):
        for u in range(UNROLL):
            slot = g * UNROLL + u
            pos = pos_ref[slot]
            row, col = pos // n_tiles, pos % n_tiles
            source, target = (col, row) if rows_out else (row, col)
            source = jnp.where(slot < count, source, n_tiles)
            rhs = jnp.concatenate(split(tile_ref[slot]), axis=1 if rows_out else 0)
            both = lax.dot_general(
                lhs_ref[source],
                rhs,
                BY_COLS if rows_out else BY_ROWS,
                preferred_element_type=jnp.float32,
            )
            out_ref[target] += both[:vecs] + both[vecs:]
        return carry

    lax.fori_loop(0, tile_ref.shape[0] // UNROLL, group, 0)


def product(rows_out, pos, count, x, tiles):
    n_tiles, vecs, width = x.shape
    smem = pl.BlockSpec(memory_space=pltpu.SMEM)
    vmem = pl.BlockSpec(memory_space=pltpu.VMEM)
    return pl.pallas_call(
        functools.partial(product_body, rows_out),
        out_shape=jax.ShapeDtypeStruct(x.shape, jnp.float32),
        in_specs=[smem, smem, vmem, vmem],
        out_specs=vmem,
        scratch_shapes=[pltpu.VMEM((n_tiles + 1, 2 * vecs, 2 * width), jnp.bfloat16)],
        compiler_params=pltpu.CompilerParams(vmem_limit_bytes=20 << 20),
        cost_estimate=pl.CostEstimate(
            flops=6 * vecs * tiles.size, bytes_accessed=4 * tiles.size, transcendentals=0
        ),
        name="row_terms" if rows_out else "col_terms",
    )(pos, count, x, tiles)


def local(vectors, tile_blocks, coords, counts):
    n_row = lax.axis_size("row")
    n_col = lax.axis_size("col")
    max_slots = tile_blocks.shape[2]
    vecs, tile = vectors.shape
    axes = ("row", "col")
    out_pairs = pairs(OUT_TURN, n_row, n_col)
    in_pairs = [(b, a) for a, b in pairs(IN_TURN, n_row, n_col)]
    tiles = tile_blocks.reshape(max_slots, tile, tile)
    pos = coords.reshape(max_slots)
    count = counts.reshape(1)

    spread = jnp.broadcast_to(vectors[None], (n_row, vecs, tile))
    x_col = lax.all_to_all(spread, "row", 0, 0, tiled=True)
    x_row = lax.ppermute(x_col, axes, in_pairs)
    row_terms = product(True, pos, count, x_col, tiles)
    moved = lax.ppermute(row_terms, axes, out_pairs)
    col_terms = product(False, pos, count, x_row, tiles)
    parts = lax.all_to_all(col_terms + moved, "row", 0, 0, tiled=True)
    return jnp.sum(parts, axis=0)


def solution(mesh):
    return jax.shard_map(
        local,
        mesh=mesh,
        in_specs=(
            P(None, ("col", "row")),
            P("row", "col", None, None, None),
            P("row", "col", None),
            P("row", "col"),
        ),
        out_specs=P(None, ("col", "row")),
        check_vma=False,
    )
```

```python
import functools

import jax
import jax.numpy as jnp
from jax import lax
from jax.experimental import pallas as pl
from jax.experimental.pallas import tpu as pltpu
from jax.sharding import PartitionSpec as P


CHUNK = 16
BY_ROWS = (((1,), (0,)), ((), ()))
BY_COLS = (((1,), (1,)), ((), ()))

TURN = (4, 6, 12, 2, 0, 11, 8, 14, 5, 3, 1, 15, 13, 10, 9, 7)


def turned(r, entry):
    c = ((((r >> 1) + (entry >> 1)) & 7) << 1) | ((r ^ entry) & 1)
    step = TURN[entry]
    half = (r >> 3) ^ ((step >> 1) & 1)
    i = (half << 3) | ((((r >> 1) + (step >> 2)) & 3) << 1) | (step & 1)
    return c, i


def pairs(n_row, n_col):
    found = []
    for r in range(n_row):
        for entry in range(n_col):
            c, i = turned(r, entry)
            found.append((r * n_col + c, i * n_col + r))
    return found


def split(value):
    high = value.astype(jnp.bfloat16)
    low = (value - high.astype(jnp.float32)).astype(jnp.bfloat16)
    return high, low


def product_body(rows_out, pos_ref, count_ref, x_ref, tile_ref, out_ref, lhs_ref, place_ref, held, done):
    n_tiles, vecs, _ = x_ref.shape

    def fetch(g):
        part = pl.ds(g * CHUNK, CHUNK)
        return pltpu.make_async_copy(tile_ref.at[part], held.at[part], done.at[g])

    count = count_ref[0]
    groups = (count + CHUNK - 1) // CHUNK

    def begin(g, carry):
        fetch(g).start()
        return carry

    lax.fori_loop(0, groups, begin, 0)
    if rows_out:
        r = lax.axis_index("row")
        for entry in range(n_tiles):
            c, i = turned(r, entry)
            place_ref[i] = c
    for t in range(n_tiles):
        high, low = split(x_ref[t])
        upper = jnp.concatenate([high, high], axis=1)
        lower = jnp.concatenate([low, jnp.zeros_like(low)], axis=1)
        lhs_ref[t] = jnp.concatenate([upper, lower], axis=0)
    lhs_ref[n_tiles] = jnp.zeros(lhs_ref.shape[1:], jnp.bfloat16)
    out_ref[...] = jnp.zeros_like(out_ref)

    def group(g, carry):
        fetch(g).wait()
        for u in range(CHUNK):
            slot = g * CHUNK + u
            pos = pos_ref[slot]
            row, col = pos // n_tiles, pos % n_tiles
            source, target = (col, row) if rows_out else (row, col)
            target = place_ref[target] if rows_out else target
            source = jnp.where(slot < count, source, n_tiles)
            rhs = jnp.concatenate(split(held[slot]), axis=1 if rows_out else 0)
            both = lax.dot_general(
                lhs_ref[source],
                rhs,
                BY_COLS if rows_out else BY_ROWS,
                preferred_element_type=jnp.float32,
            )
            out_ref[target] += both[:vecs] + both[vecs:]
        return carry

    lax.fori_loop(0, groups, group, 0)


def product(rows_out, pos, count, x, tiles):
    n_tiles, vecs, width = x.shape
    smem = pl.BlockSpec(memory_space=pltpu.SMEM)
    vmem = pl.BlockSpec(memory_space=pltpu.VMEM)
    return pl.pallas_call(
        functools.partial(product_body, rows_out),
        out_shape=jax.ShapeDtypeStruct(x.shape, jnp.float32),
        in_specs=[smem, smem, vmem, pl.BlockSpec(memory_space=pltpu.HBM)],
        out_specs=vmem,
        scratch_shapes=[
            pltpu.VMEM((n_tiles + 1, 2 * vecs, 2 * width), jnp.bfloat16),
            pltpu.SMEM((n_tiles,), jnp.int32),
            pltpu.VMEM(tiles.shape, tiles.dtype),
            pltpu.SemaphoreType.DMA((tiles.shape[0] // CHUNK,)),
        ],
        compiler_params=pltpu.CompilerParams(vmem_limit_bytes=53 << 20),
        cost_estimate=pl.CostEstimate(
            flops=6 * vecs * tiles.size, bytes_accessed=4 * tiles.size, transcendentals=0
        ),
        name="row_terms" if rows_out else "col_terms",
    )(pos, count, x, tiles)


def local(vectors, tile_blocks, coords, counts):
    n_row = lax.axis_size("row")
    n_col = lax.axis_size("col")
    max_slots = tile_blocks.shape[2]
    vecs, tile = vectors.shape
    axes = ("row", "col")
    turn = pairs(n_row, n_col)
    tiles = tile_blocks.reshape(max_slots, tile, tile)
    pos = coords.reshape(max_slots)
    count = counts.reshape(1)

    spread = jnp.broadcast_to(vectors[None], (n_row, vecs, tile))
    x_col = lax.all_to_all(spread, "row", 0, 0, tiled=True)
    x_row = lax.ppermute(x_col, axes, [(b, a) for a, b in turn])
    row_terms = product(True, pos, count, x_col, tiles)
    row_parts = lax.all_to_all(row_terms, "col", 0, 0, tiled=True)
    col_terms = product(False, pos, count, x_row, tiles)
    col_parts = lax.all_to_all(col_terms, "row", 0, 0, tiled=True)
    row_sum = lax.ppermute(jnp.sum(row_parts, axis=0), axes, turn)
    return jnp.sum(col_parts, axis=0) + row_sum


def solution(mesh):
    return jax.shard_map(
        local,
        mesh=mesh,
        in_specs=(
            P(None, ("col", "row")),
            P("row", "col", None, None, None),
            P("row", "col", None),
            P("row", "col"),
        ),
        out_specs=P(None, ("col", "row")),
        check_vma=False,
    )
```

```python
import functools

import jax
import jax.numpy as jnp
from jax import lax
from jax.experimental import pallas as pl
from jax.experimental.pallas import tpu as pltpu
from jax.sharding import PartitionSpec as P


CHUNK = 16
BY_ROWS = (((1,), (0,)), ((), ()))
BY_COLS = (((1,), (1,)), ((), ()))

TURN = (4, 6, 12, 2, 0, 11, 8, 14, 5, 3, 1, 15, 13, 10, 9, 7)


def turned(r, entry):
    c = ((((r >> 1) + (entry >> 1)) & 7) << 1) | ((r ^ entry) & 1)
    step = TURN[entry]
    half = (r >> 3) ^ ((step >> 1) & 1)
    i = (half << 3) | ((((r >> 1) + (step >> 2)) & 3) << 1) | (step & 1)
    return c, i


def pairs(n_row, n_col):
    found = []
    for r in range(n_row):
        for entry in range(n_col):
            c, i = turned(r, entry)
            found.append((r * n_col + c, i * n_col + r))
    return found


def split(value):
    high = value.astype(jnp.bfloat16)
    low = (value - high.astype(jnp.float32)).astype(jnp.bfloat16)
    return high, low


def product_body(
    rows_out, plan, count_ref, x_ref, tiles, out_ref, lhs_ref, place_ref, held, pos_ref, done
):
    n_tiles, vecs, _ = x_ref.shape
    bits = n_tiles.bit_length() - 1
    count = count_ref[0, 0]
    groups = lax.div(count + (CHUNK - 1), CHUNK)
    pos_copy = pltpu.make_async_copy(plan, pos_ref, done.at[held.shape[0] // CHUNK])
    pos_copy.start()

    def fetch(g):
        part = pl.ds(g * CHUNK, CHUNK)
        return pltpu.make_async_copy(tiles.at[part], held.at[part], done.at[g])

    def ask(g, carry):
        fetch(g).start()
        return carry

    lax.fori_loop(0, groups, ask, 0)
    if rows_out:
        r = lax.axis_index("row")
        for entry in range(n_tiles):
            c, i = turned(r, entry)
            place_ref[i] = c
    for t in range(n_tiles):
        high, low = split(x_ref[t])
        upper = jnp.concatenate([high, high], axis=1)
        lower = jnp.concatenate([low, jnp.zeros_like(low)], axis=1)
        lhs_ref[t] = jnp.concatenate([upper, lower], axis=0)
    lhs_ref[n_tiles] = jnp.zeros(lhs_ref.shape[1:], jnp.bfloat16)
    out_ref[...] = jnp.zeros_like(out_ref)
    pos_copy.wait()

    def group(g, carry):
        fetch(g).wait()
        for u in range(CHUNK):
            slot = g * CHUNK + u
            pos = pos_ref[0, 0, slot]
            row, col = lax.shift_right_logical(pos, bits), lax.bitwise_and(pos, n_tiles - 1)
            source, target = (col, place_ref[row]) if rows_out else (row, col)
            source = jnp.where(slot < count, source, n_tiles)
            rhs = jnp.concatenate(split(held[slot]), axis=1 if rows_out else 0)
            both = lax.dot_general(
                lhs_ref[source],
                rhs,
                BY_COLS if rows_out else BY_ROWS,
                preferred_element_type=jnp.float32,
            )
            out_ref[target] += both[:vecs] + both[vecs:]
        return carry

    lax.fori_loop(0, groups, group, 0)


def product(rows_out, plan, count, x, tiles):
    n_tiles, vecs, width = x.shape
    anywhere = pl.BlockSpec(memory_space=pl.ANY)
    smem = pl.BlockSpec(memory_space=pltpu.SMEM)
    vmem = pl.BlockSpec(memory_space=pltpu.VMEM)
    return pl.pallas_call(
        functools.partial(product_body, rows_out),
        out_shape=jax.ShapeDtypeStruct(x.shape, jnp.float32),
        in_specs=[anywhere, smem, vmem, anywhere],
        out_specs=vmem,
        scratch_shapes=[
            pltpu.VMEM((n_tiles + 1, 2 * vecs, 2 * width), jnp.bfloat16),
            pltpu.SMEM((n_tiles,), jnp.int32),
            pltpu.VMEM(tiles.shape, tiles.dtype),
            pltpu.SMEM(plan.shape, plan.dtype),
            pltpu.SemaphoreType.DMA((tiles.shape[0] // CHUNK + 1,)),
        ],
        compiler_params=pltpu.CompilerParams(vmem_limit_bytes=53 << 20),
        cost_estimate=pl.CostEstimate(
            flops=6 * vecs * tiles.size, bytes_accessed=4 * tiles.size, transcendentals=0
        ),
        name="row_terms" if rows_out else "col_terms",
    )(plan, count, x, tiles)


def begin_body(count_ref, coords_ref, x_ref, out_ref, plan_ref):
    plan_ref[...] = coords_ref[...]
    out_ref[...] = jnp.broadcast_to(x_ref[...][None], out_ref.shape)


def begin(count, coords, x, n_copies):
    vmem = pl.BlockSpec(memory_space=pltpu.VMEM)
    return pl.pallas_call(
        begin_body,
        out_shape=(
            jax.ShapeDtypeStruct((n_copies, *x.shape), x.dtype),
            jax.ShapeDtypeStruct(coords.shape, coords.dtype),
        ),
        in_specs=[pl.BlockSpec(memory_space=pltpu.SMEM), vmem, vmem],
        out_specs=(vmem, vmem),
        compiler_params=pltpu.CompilerParams(vmem_limit_bytes=4 << 20),
        name="begin",
    )(count, coords, x)


def local(vectors, tile_blocks, coords, counts):
    n_row = lax.axis_size("row")
    n_col = lax.axis_size("col")
    max_slots = tile_blocks.shape[2]
    _, tile = vectors.shape
    axes = ("row", "col")
    turn = pairs(n_row, n_col)
    tiles = tile_blocks.reshape(max_slots, tile, tile)

    spread, plan = begin(counts, coords, vectors, n_row)
    x_col = lax.all_to_all(spread, "row", 0, 0, tiled=True)
    x_row = lax.ppermute(x_col, axes, [(b, a) for a, b in turn])
    row_terms = product(True, plan, counts, x_col, tiles)
    row_parts = lax.all_to_all(row_terms, "col", 0, 0, tiled=True)
    col_terms = product(False, plan, counts, x_row, tiles)
    col_parts = lax.all_to_all(col_terms, "row", 0, 0, tiled=True)
    row_sum = lax.ppermute(jnp.sum(row_parts, axis=0), axes, turn)
    return jnp.sum(col_parts, axis=0) + row_sum


def solution(mesh):
    return jax.shard_map(
        local,
        mesh=mesh,
        in_specs=(
            P(None, ("col", "row")),
            P("row", "col", None, None, None),
            P("row", "col", None),
            P("row", "col"),
        ),
        out_specs=P(None, ("col", "row")),
        check_vma=False,
    )
```

```python
import functools

import jax
import jax.numpy as jnp
from jax import lax
from jax.experimental import pallas as pl
from jax.experimental.pallas import tpu as pltpu
from jax.sharding import PartitionSpec as P


CHUNK = 16
BY_ROWS = (((1,), (0,)), ((), ()))
BY_COLS = (((1,), (1,)), ((), ()))

TURN = (4, 6, 12, 2, 0, 11, 8, 14, 5, 3, 1, 15, 13, 10, 9, 7)


def turned(r, entry):
    c = ((((r >> 1) + (entry >> 1)) & 7) << 1) | ((r ^ entry) & 1)
    step = TURN[entry]
    half = (r >> 3) ^ ((step >> 1) & 1)
    i = (half << 3) | ((((r >> 1) + (step >> 2)) & 3) << 1) | (step & 1)
    return c, i


def pairs(n_row, n_col):
    found = []
    for r in range(n_row):
        for entry in range(n_col):
            c, i = turned(r, entry)
            found.append((r * n_col + c, i * n_col + r))
    return found


def split(value):
    high = value.astype(jnp.bfloat16)
    low = (value - high.astype(jnp.float32)).astype(jnp.bfloat16)
    return high, low


def product_body(
    rows_out, plan, count_ref, x_ref, tiles, out_ref, lhs_ref, place_ref, held, pos_ref, done
):
    n_tiles, vecs, _ = x_ref.shape
    bits = n_tiles.bit_length() - 1
    count = count_ref[0, 0]
    groups = lax.div(count + (CHUNK - 1), CHUNK)
    pos_copy = pltpu.make_async_copy(plan, pos_ref, done.at[held.shape[0] // CHUNK])
    pos_copy.start()

    def fetch(g):
        part = pl.ds(g * CHUNK, CHUNK)
        return pltpu.make_async_copy(tiles.at[part], held.at[part], done.at[g])

    def ask(g, carry):
        fetch(g).start()
        return carry

    lax.fori_loop(0, groups, ask, 0)
    if rows_out:
        r = lax.axis_index("row")
        for entry in range(n_tiles):
            c, i = turned(r, entry)
            place_ref[i] = c
    for t in range(n_tiles):
        high, low = split(x_ref[t])
        upper = jnp.concatenate([high, high], axis=1)
        lower = jnp.concatenate([low, jnp.zeros_like(low)], axis=1)
        lhs_ref[t] = jnp.concatenate([upper, lower], axis=0)
    lhs_ref[n_tiles] = jnp.zeros(lhs_ref.shape[1:], jnp.bfloat16)
    out_ref[...] = jnp.zeros_like(out_ref)
    pos_copy.wait()

    def group(g, carry):
        fetch(g).wait()
        for u in range(CHUNK):
            slot = g * CHUNK + u
            pos = pos_ref[0, 0, slot]
            row = lax.bitwise_and(lax.shift_right_logical(pos, bits), n_tiles - 1)
            col = lax.bitwise_and(pos, n_tiles - 1)
            source, target = (col, place_ref[row]) if rows_out else (row, col)
            source = jnp.where(pos < 0, n_tiles, source)
            rhs = jnp.concatenate(split(held[slot]), axis=1 if rows_out else 0)
            both = lax.dot_general(
                lhs_ref[source],
                rhs,
                BY_COLS if rows_out else BY_ROWS,
                preferred_element_type=jnp.float32,
            )
            out_ref[target] += both[:vecs] + both[vecs:]
        return carry

    lax.fori_loop(0, groups, group, 0)


def product(rows_out, plan, count, x, tiles):
    n_tiles, vecs, width = x.shape
    anywhere = pl.BlockSpec(memory_space=pl.ANY)
    smem = pl.BlockSpec(memory_space=pltpu.SMEM)
    vmem = pl.BlockSpec(memory_space=pltpu.VMEM)
    return pl.pallas_call(
        functools.partial(product_body, rows_out),
        out_shape=jax.ShapeDtypeStruct(x.shape, jnp.float32),
        in_specs=[anywhere, smem, vmem, anywhere],
        out_specs=vmem,
        scratch_shapes=[
            pltpu.VMEM((n_tiles + 1, 2 * vecs, 2 * width), jnp.bfloat16),
            pltpu.SMEM((n_tiles,), jnp.int32),
            pltpu.VMEM(tiles.shape, tiles.dtype),
            pltpu.SMEM(plan.shape, plan.dtype),
            pltpu.SemaphoreType.DMA((tiles.shape[0] // CHUNK + 1,)),
        ],
        compiler_params=pltpu.CompilerParams(vmem_limit_bytes=53 << 20),
        cost_estimate=pl.CostEstimate(
            flops=6 * vecs * tiles.size, bytes_accessed=4 * tiles.size, transcendentals=0
        ),
        name="row_terms" if rows_out else "col_terms",
    )(plan, count, x, tiles)


def local(vectors, tile_blocks, coords, counts):
    n_row = lax.axis_size("row")
    n_col = lax.axis_size("col")
    max_slots = tile_blocks.shape[2]
    vecs, tile = vectors.shape
    axes = ("row", "col")
    turn = pairs(n_row, n_col)
    tiles = tile_blocks.reshape(max_slots, tile, tile)

    spread = jnp.broadcast_to(vectors[None], (n_row, vecs, tile))
    slots = jnp.arange(max_slots, dtype=jnp.int32)
    plan = jnp.where(slots < counts[:, :, None], coords, -1)
    x_col = lax.all_to_all(spread, "row", 0, 0, tiled=True)
    x_row = lax.ppermute(x_col, axes, [(b, a) for a, b in turn])
    row_terms = product(True, plan, counts, x_col, tiles)
    row_parts = lax.all_to_all(row_terms, "col", 0, 0, tiled=True)
    col_terms = product(False, plan, counts, x_row, tiles)
    col_parts = lax.all_to_all(col_terms, "row", 0, 0, tiled=True)
    row_sum = lax.ppermute(jnp.sum(row_parts, axis=0), axes, turn)
    return jnp.sum(col_parts, axis=0) + row_sum


def solution(mesh):
    return jax.shard_map(
        local,
        mesh=mesh,
        in_specs=(
            P(None, ("col", "row")),
            P("row", "col", None, None, None),
            P("row", "col", None),
            P("row", "col"),
        ),
        out_specs=P(None, ("col", "row")),
        check_vma=False,
    )
```

```python
import jax
import jax.numpy as jnp
from jax import lax
from jax.experimental import pallas as pl
from jax.experimental.pallas import tpu as pltpu
from jax.sharding import PartitionSpec as P


CHUNK = 16
BY_ROWS = (((1,), (0,)), ((), ()))
BY_COLS = (((1,), (1,)), ((), ()))

TURN_IN = (4, 6, 12, 2, 0, 11, 8, 14, 5, 3, 1, 15, 13, 10, 9, 7)
TURN_OUT = (4, 2, 0, 10, 1, 6, 9, 14, 13, 3, 8, 15, 5, 7, 12, 11)


def turned(turn, r, entry):
    c = ((((r >> 1) + (entry >> 1)) & 7) << 1) | ((r ^ entry) & 1)
    step = turn[entry]
    half = (r >> 3) ^ ((step >> 1) & 1)
    i = (half << 3) | ((((r >> 1) + (step >> 2)) & 3) << 1) | (step & 1)
    return c, i


def pairs(turn, n_row, n_col):
    found = []
    for r in range(n_row):
        for entry in range(n_col):
            c, i = turned(turn, r, entry)
            found.append((r * n_col + c, i * n_col + r))
    return found


def parity(turn, i, r):
    odd = sum((entry & 1) << step for entry, step in enumerate(turn))
    step = ((((i >> 1) - (r >> 1)) & 3) << 2) | (((i ^ r) >> 3) << 1) | (i & 1)
    return ((odd >> step) ^ r) & 1


def split(value):
    high = value.astype(jnp.bfloat16)
    low = (value - high.astype(jnp.float32)).astype(jnp.bfloat16)
    return high, low


def accumulate(rows_out, plan, count_ref, tiles, acc_ref, lhs_ref, held, pos_ref, done, x_parts):
    n_tiles, vecs, _ = acc_ref.shape
    bits = n_tiles.bit_length() - 1
    n_half = n_tiles // 2
    side = lax.bitwise_and(lax.axis_index("col"), 1)
    count = count_ref[0, 0]
    groups = lax.div(count + (CHUNK - 1), CHUNK)
    pos_copy = pltpu.make_async_copy(plan, pos_ref, done.at[held.shape[0] // CHUNK])
    pos_copy.start()

    def fetch(g):
        part = pl.ds(g * CHUNK, CHUNK)
        return pltpu.make_async_copy(tiles.at[part], held.at[part], done.at[g])

    def ask(g, carry):
        fetch(g).start()
        return carry

    lax.fori_loop(0, groups, ask, 0)
    first = 0
    for x_ref in x_parts:
        for t in range(x_ref.shape[0]):
            high, low = split(x_ref[t])
            upper = jnp.concatenate([high, high], axis=1)
            lower = jnp.concatenate([low, jnp.zeros_like(low)], axis=1)
            lhs_ref[first + t] = jnp.concatenate([upper, lower], axis=0)
        first += x_ref.shape[0]
    lhs_ref[n_tiles] = jnp.zeros(lhs_ref.shape[1:], jnp.bfloat16)
    acc_ref[...] = jnp.zeros_like(acc_ref)
    pos_copy.wait()

    def group(g, carry):
        fetch(g).wait()
        for u in range(CHUNK):
            slot = g * CHUNK + u
            pos = pos_ref[0, 0, slot]
            row = lax.bitwise_and(lax.shift_right_logical(pos, bits), n_tiles - 1)
            row = lax.bitwise_xor(row, side * n_half) if rows_out else row
            col = lax.bitwise_and(pos, n_tiles - 1)
            source, target = (col, row) if rows_out else (row, col)
            source = jnp.where(pos < 0, n_tiles, source)
            rhs = jnp.concatenate(split(held[slot]), axis=1 if rows_out else 0)
            both = lax.dot_general(
                lhs_ref[source],
                rhs,
                BY_COLS if rows_out else BY_ROWS,
                preferred_element_type=jnp.float32,
            )
            acc_ref[target] += both[:vecs] + both[vecs:]
        return carry

    lax.fori_loop(0, groups, group, 0)


def rows_body(plan, count_ref, x_ref, tiles, keep_ref, send_ref, acc_ref, *rest):
    accumulate(True, plan, count_ref, tiles, acc_ref, *rest, [x_ref])
    n_half = keep_ref.shape[0]
    keep_ref[...] = acc_ref[:n_half]
    send_ref[...] = acc_ref[n_half:]


def cols_body(plan, count_ref, x_ref, tiles, out_ref, *rest):
    accumulate(False, plan, count_ref, tiles, out_ref, *rest, [x_ref])


def product(rows_out, plan, count, x_parts, tiles):
    _, vecs, width = x_parts[0].shape
    n_tiles = sum(x.shape[0] for x in x_parts)
    anywhere = pl.BlockSpec(memory_space=pl.ANY)
    smem = pl.BlockSpec(memory_space=pltpu.SMEM)
    vmem = pl.BlockSpec(memory_space=pltpu.VMEM)
    whole, half = (n_tiles, vecs, width), (n_tiles // 2, vecs, width)
    out = jax.ShapeDtypeStruct(half if rows_out else whole, jnp.float32)
    acc = [pltpu.VMEM(whole, jnp.float32)] if rows_out else []
    return pl.pallas_call(
        rows_body if rows_out else cols_body,
        out_shape=(out, out) if rows_out else out,
        in_specs=[anywhere, smem, *[vmem] * len(x_parts), anywhere],
        out_specs=(vmem, vmem) if rows_out else vmem,
        scratch_shapes=[
            *acc,
            pltpu.VMEM((n_tiles + 1, 2 * vecs, 2 * width), jnp.bfloat16),
            pltpu.VMEM(tiles.shape, tiles.dtype),
            pltpu.SMEM(plan.shape, plan.dtype),
            pltpu.SemaphoreType.DMA((tiles.shape[0] // CHUNK + 1,)),
        ],
        compiler_params=pltpu.CompilerParams(vmem_limit_bytes=53 << 20),
        cost_estimate=pl.CostEstimate(
            flops=6 * vecs * tiles.size, bytes_accessed=4 * tiles.size, transcendentals=0
        ),
        name="row_terms" if rows_out else "col_terms",
    )(plan, count, *x_parts, tiles)


def local(vectors, tile_blocks, coords, counts):
    n_row = lax.axis_size("row")
    n_col = lax.axis_size("col")
    max_slots = tile_blocks.shape[2]
    vecs, tile = vectors.shape
    axes = ("row", "col")
    n_half = n_row // 2
    in_pairs = pairs(TURN_IN, n_row, n_col)
    out_pairs = pairs(TURN_OUT, n_row, n_col)
    swap = [(c, c ^ 1) for c in range(n_col)]
    tiles = tile_blocks.reshape(max_slots, tile, tile)
    spread = jnp.broadcast_to(vectors[None], (n_row, vecs, tile))
    slots = jnp.arange(max_slots, dtype=jnp.int32)
    plan = jnp.where(slots < counts[:, :, None], coords, -1)
    side = parity(TURN_OUT, lax.axis_index("row"), lax.axis_index("col"))
    x_col = lax.all_to_all(spread, "row", 0, 0, tiled=True)
    x_row = lax.ppermute(x_col, axes, [(b, a) for a, b in in_pairs])
    keep, send = product(True, plan, counts, [x_col], tiles)
    got = lax.ppermute(send, "col", swap)
    moved = lax.ppermute(keep + got, axes, out_pairs)
    col_terms = product(False, plan, counts, [x_row], tiles)
    base = side * n_half
    mine = lax.dynamic_slice_in_dim(col_terms, base, n_half, 0) + moved
    both = lax.dynamic_update_slice_in_dim(col_terms, mine, base, 0)
    col_parts = lax.all_to_all(both, "row", 0, 0, tiled=True)
    return jnp.sum(col_parts, axis=0)


def solution(mesh):
    return jax.shard_map(
        local,
        mesh=mesh,
        in_specs=(
            P(None, ("col", "row")),
            P("row", "col", None, None, None),
            P("row", "col", None),
            P("row", "col"),
        ),
        out_specs=P(None, ("col", "row")),
        check_vma=False,
    )
```

```python
import jax
import jax.numpy as jnp
from jax import lax
from jax.experimental import pallas as pl
from jax.experimental.pallas import tpu as pltpu
from jax.sharding import PartitionSpec as P


CHUNK = 16
BY_ROWS = (((1,), (0,)), ((), ()))
BY_COLS = (((1,), (1,)), ((), ()))

TURN = (12, 11, 5, 10, 8, 14, 0, 6, 13, 3, 4, 2, 1, 15, 9, 7)


def turned(turn, r, entry):
    c = ((((r >> 1) + (entry >> 1)) & 7) << 1) | ((r ^ entry) & 1)
    step = turn[entry]
    half = (r >> 3) ^ ((step >> 1) & 1)
    i = (half << 3) | ((((r >> 1) + (step >> 2)) & 3) << 1) | (step & 1)
    return c, i


def pairs(turn, n_row, n_col):
    found = []
    for r in range(n_row):
        for entry in range(n_col):
            c, i = turned(turn, r, entry)
            found.append((r * n_col + c, i * n_col + r))
    return found


def parity(turn, i, r):
    odd = sum((entry & 1) << step for entry, step in enumerate(turn))
    step = ((((i >> 1) - (r >> 1)) & 3) << 2) | (((i ^ r) >> 3) << 1) | (i & 1)
    return ((odd >> step) ^ r) & 1


def split(value):
    high = value.astype(jnp.bfloat16)
    low = (value - high.astype(jnp.float32)).astype(jnp.bfloat16)
    return high, low


def accumulate(rows_out, plan, count_ref, tiles, acc_ref, lhs_ref, held, pos_ref, done, x_parts):
    n_tiles, vecs, _ = acc_ref.shape
    bits = n_tiles.bit_length() - 1
    n_half = n_tiles // 2
    side = lax.bitwise_and(lax.axis_index("col"), 1)
    count = count_ref[0, 0]
    groups = lax.div(count + (CHUNK - 1), CHUNK)
    pos_copy = pltpu.make_async_copy(plan, pos_ref, done.at[held.shape[0] // CHUNK])
    pos_copy.start()

    def fetch(g):
        part = pl.ds(g * CHUNK, CHUNK)
        return pltpu.make_async_copy(tiles.at[part], held.at[part], done.at[g])

    def ask(g, carry):
        fetch(g).start()
        return carry

    lax.fori_loop(0, groups, ask, 0)
    first = 0
    for x_ref in x_parts:
        for t in range(x_ref.shape[0]):
            high, low = split(x_ref[t])
            upper = jnp.concatenate([high, high], axis=1)
            lower = jnp.concatenate([low, jnp.zeros_like(low)], axis=1)
            lhs_ref[first + t] = jnp.concatenate([upper, lower], axis=0)
        first += x_ref.shape[0]
    lhs_ref[n_tiles] = jnp.zeros(lhs_ref.shape[1:], jnp.bfloat16)
    acc_ref[...] = jnp.zeros_like(acc_ref)
    pos_copy.wait()

    def group(g, carry):
        fetch(g).wait()
        for u in range(CHUNK):
            slot = g * CHUNK + u
            pos = pos_ref[0, 0, slot]
            row = lax.bitwise_and(lax.shift_right_logical(pos, bits), n_tiles - 1)
            row = lax.bitwise_xor(row, side * n_half) if rows_out else row
            col = lax.bitwise_and(pos, n_tiles - 1)
            source, target = (col, row) if rows_out else (row, col)
            source = jnp.where(pos < 0, n_tiles, source)
            rhs = jnp.concatenate(split(held[slot]), axis=1 if rows_out else 0)
            both = lax.dot_general(
                lhs_ref[source],
                rhs,
                BY_COLS if rows_out else BY_ROWS,
                preferred_element_type=jnp.float32,
            )
            acc_ref[target] += both[:vecs] + both[vecs:]
        return carry

    lax.fori_loop(0, groups, group, 0)


def rows_body(plan, count_ref, x_ref, tiles, keep_ref, send_ref, acc_ref, *rest):
    accumulate(True, plan, count_ref, tiles, acc_ref, *rest, [x_ref])
    n_half = keep_ref.shape[0]
    keep_ref[...] = acc_ref[:n_half]
    send_ref[...] = acc_ref[n_half:]


def cols_body(plan, count_ref, x_ref, tiles, out_ref, *rest):
    accumulate(False, plan, count_ref, tiles, out_ref, *rest, [x_ref])


def product(rows_out, plan, count, x_parts, tiles):
    _, vecs, width = x_parts[0].shape
    n_tiles = sum(x.shape[0] for x in x_parts)
    anywhere = pl.BlockSpec(memory_space=pl.ANY)
    smem = pl.BlockSpec(memory_space=pltpu.SMEM)
    vmem = pl.BlockSpec(memory_space=pltpu.VMEM)
    whole, half = (n_tiles, vecs, width), (n_tiles // 2, vecs, width)
    out = jax.ShapeDtypeStruct(half if rows_out else whole, jnp.float32)
    acc = [pltpu.VMEM(whole, jnp.float32)] if rows_out else []
    return pl.pallas_call(
        rows_body if rows_out else cols_body,
        out_shape=(out, out) if rows_out else out,
        in_specs=[anywhere, smem, *[vmem] * len(x_parts), anywhere],
        out_specs=(vmem, vmem) if rows_out else vmem,
        scratch_shapes=[
            *acc,
            pltpu.VMEM((n_tiles + 1, 2 * vecs, 2 * width), jnp.bfloat16),
            pltpu.VMEM(tiles.shape, tiles.dtype),
            pltpu.SMEM(plan.shape, plan.dtype),
            pltpu.SemaphoreType.DMA((tiles.shape[0] // CHUNK + 1,)),
        ],
        compiler_params=pltpu.CompilerParams(vmem_limit_bytes=53 << 20),
        cost_estimate=pl.CostEstimate(
            flops=6 * vecs * tiles.size, bytes_accessed=4 * tiles.size, transcendentals=0
        ),
        name="row_terms" if rows_out else "col_terms",
    )(plan, count, *x_parts, tiles)


def local(vectors, tile_blocks, coords, counts):
    n_row = lax.axis_size("row")
    n_col = lax.axis_size("col")
    max_slots = tile_blocks.shape[2]
    vecs, tile = vectors.shape
    axes = ("row", "col")
    n_half = n_row // 2
    out_pairs = pairs(TURN, n_row, n_col)
    in_pairs = [(b, a) for a, b in out_pairs]
    swap = [(c, c ^ 1) for c in range(n_col)]
    tiles = tile_blocks.reshape(max_slots, tile, tile)
    spread = jnp.broadcast_to(vectors[None], (n_row, vecs, tile))
    slots = jnp.arange(max_slots, dtype=jnp.int32)
    plan = jnp.where(slots < counts[:, :, None], coords, -1)
    side = parity(TURN, lax.axis_index("row"), lax.axis_index("col"))
    x_col = lax.all_to_all(spread, "row", 0, 0, tiled=True)
    x_row = lax.ppermute(x_col, axes, in_pairs)
    keep, send = product(True, plan, counts, [x_col], tiles)
    got = lax.ppermute(send, "col", swap)
    moved = lax.ppermute(keep + got, axes, out_pairs)
    col_terms = product(False, plan, counts, [x_row], tiles)
    base = side * n_half
    mine = lax.dynamic_slice_in_dim(col_terms, base, n_half, 0) + moved
    both = lax.dynamic_update_slice_in_dim(col_terms, mine, base, 0)
    col_parts = lax.all_to_all(both, "row", 0, 0, tiled=True)
    return jnp.sum(col_parts, axis=0)


def solution(mesh):
    return jax.shard_map(
        local,
        mesh=mesh,
        in_specs=(
            P(None, ("col", "row")),
            P("row", "col", None, None, None),
            P("row", "col", None),
            P("row", "col"),
        ),
        out_specs=P(None, ("col", "row")),
        check_vma=False,
    )
```
